128 devices in a mesh: rep: 8 (over z, core), shard: 16 (over x, y).
Axes of the slice: x: 4, y: 4, z: 4, core: 2. Of those that a mesh axis runs over, the one named last changes fastest.
Arguments:
- inputs: bfloat16 [16384, 1152], P(('rep', 'shard')), may hold values from -6 to 6
- lengths: int32 [128, 2], P(('rep', 'shard')), may hold values from 1 to 64, as said below
- q_weight: bfloat16 [1152, 1024], P('shard'), may hold values from -0.1875 to 0.1875
- k_weight: bfloat16 [1152, 256], P('shard'), may hold values from -0.1875 to 0.1875
- v_weight: bfloat16 [1152, 256], P('shard'), may hold values from -0.1875 to 0.1875
- o_weight: bfloat16 [1152, 1024], P('shard'), may hold values from -0.1875 to 0.1875
- gate_weight: bfloat16 [1152, 6912], P('shard'), may hold values from -0.1875 to 0.1875
- up_weight: bfloat16 [1152, 6912], P('shard'), may hold values from -0.1875 to 0.1875
- down_weight: bfloat16 [1152, 6912], P('shard'), may hold values from -0.078125 to 0.078125
- attn_norm: bfloat16 [1152], P('shard'), may hold values from 0.5 to 1.5
- attn_post_norm: bfloat16 [1152], P('shard'), may hold values from 0.5 to 1.5
- mlp_norm: bfloat16 [1152], P('shard'), may hold values from 0.5 to 1.5
- mlp_post_norm: bfloat16 [1152], P('shard'), may hold values from 0.5 to 1.5
- query_norm: bfloat16 [256], P('shard'), may hold values from 0.5 to 1.5
- key_norm: bfloat16 [256], P('shard'), may hold values from 0.5 to 1.5
- cotangent: bfloat16 [16384, 1152], P(('rep', 'shard')), may hold values from -6 to 6
Outputs:
- outputs: bfloat16 [16384, 1152], P(('rep', 'shard'))
- input_grad: bfloat16 [16384, 1152], P(('rep', 'shard'))
- grad_q_weight: float32 [1152, 1024], P('shard')
- grad_k_weight: float32 [1152, 256], P('shard')
- grad_v_weight: float32 [1152, 256], P('shard')
- grad_o_weight: float32 [1152, 1024], P('shard')
- grad_gate_weight: float32 [1152, 6912], P('shard')
- grad_up_weight: float32 [1152, 6912], P('shard')
- grad_down_weight: float32 [1152, 6912], P('shard')
- grad_attn_norm: float32 [1152], P('shard')
- grad_attn_post_norm: float32 [1152], P('shard')
- grad_mlp_norm: float32 [1152], P('shard')
- grad_mlp_post_norm: float32 [1152], P('shard')
- grad_query_norm: float32 [256], P('shard')
- grad_key_norm: float32 [256], P('shard')
The draws below stay inside these ranges and needn't reach their ends.
Inputs may be any that keep to these rules, and one draw needn't show every extreme that they name: Each device has 2 sequence slots of 1 to 64 tokens; in every draw one device has all its lengths equal to 64, so that its 128 rows are all live.
All inputs are finite; a program needn't handle non-finite values.
Results may differ from the reference program's by a relative error of at most 0.023.
Values may be sent and summed in bfloat16 or wider, within the bound.
No kernel may reach another device: no remote copies, remote signals or barrier semaphores. Data moves between devices by JAX's collectives and lax.ppermute only.
A program may use at most 192 MiB of HBM per device.

```python
import jax
import jax.numpy as jnp
from jax import lax

D = 1152
FF = 6912
HEADS = 4
HD = 256
QW = 1024
MAXLEN = 64
SEQ_DEV = 2
TOK_DEV = 128
ROWS = 16384
DEVICES = 128


def draw_lengths(key, part):
    base = jax.random.fold_in(key, 11)
    key_dev, key_seq, key_full = jax.random.split(base, 3)
    dev_level = jax.random.randint(key_dev, (DEVICES, 1), 32, 64)
    seq_level = jax.random.randint(key_seq, (DEVICES, SEQ_DEV), 40, 64)
    drawn = 1 + dev_level * seq_level * (MAXLEN - 1) // 3969
    chosen = jax.random.randint(key_full, (), 0, DEVICES)
    device_ids = jnp.arange(DEVICES)[:, None]
    return jnp.where(device_ids == chosen, MAXLEN, drawn).astype(jnp.int32)


def levels(rng, dims, pieces, least, largest):
    level, own = 1.0, jax.random.fold_in(rng, 6)
    for dim, parts in pieces:
        steps = jnp.exp(jax.random.uniform(jax.random.fold_in(own, dim), (parts,), jnp.float32, least / len(pieces), largest / len(pieces)))
        level = level * jnp.repeat(steps, dims[dim] // parts).reshape([-1 if axis == dim else 1 for axis in range(len(dims))])
    return level


def noise(rng, extent, scale, limit, cuts=(), kind=jnp.bfloat16):
    values = jax.random.normal(rng, extent, jnp.float32) * scale
    if len(cuts) > 0:
        values = levels(rng, extent, cuts, -0.22, 0.18) * values
    return jnp.clip(values, min=-limit, max=limit).astype(kind)


def setup_inputs(seed: int = 0) -> dict:
    splits = jax.random.split(jax.random.key(seed), 17)
    return {
        "inputs": noise(splits[0], (ROWS, D), 1.0, 6.0, ((0, 128),)),
        "lengths": draw_lengths(jax.random.fold_in(splits[16], 71), 0),
        "q_weight": noise(splits[2], (D, QW), D ** -0.5, 0.1875, ((0, 16),)),
        "k_weight": noise(splits[3], (D, HD), D ** -0.5, 0.1875, ((0, 16),)),
        "v_weight": noise(splits[4], (D, HD), D ** -0.5, 0.1875, ((0, 16),)),
        "o_weight": noise(splits[5], (D, QW), QW ** -0.5, 0.1875, ((0, 16),)),
        "gate_weight": noise(splits[6], (D, FF), D ** -0.5, 0.1875, ((0, 16),)),
        "up_weight": noise(splits[7], (D, FF), D ** -0.5, 0.1875, ((0, 16),)),
        "down_weight": noise(splits[8], (D, FF), FF ** -0.5, 0.078125, ((0, 16),)),
        "attn_norm": jnp.clip(1.0 + 0.1 * jax.random.normal(splits[9], (D,), jnp.float32), 0.5, 1.5).astype(jnp.bfloat16),
        "attn_post_norm": jnp.clip(1.0 + 0.1 * jax.random.normal(splits[10], (D,), jnp.float32), 0.5, 1.5).astype(jnp.bfloat16),
        "mlp_norm": jnp.clip(1.0 + 0.1 * jax.random.normal(splits[11], (D,), jnp.float32), 0.5, 1.5).astype(jnp.bfloat16),
        "mlp_post_norm": jnp.clip(1.0 + 0.1 * jax.random.normal(splits[12], (D,), jnp.float32), 0.5, 1.5).astype(jnp.bfloat16),
        "query_norm": jnp.clip(1.0 + 0.1 * jax.random.normal(splits[13], (HD,), jnp.float32), 0.5, 1.5).astype(jnp.bfloat16),
        "key_norm": jnp.clip(1.0 + 0.1 * jax.random.normal(splits[14], (HD,), jnp.float32), 0.5, 1.5).astype(jnp.bfloat16),
        "cotangent": noise(splits[15], (ROWS, D), 1.0, 6.0, ((0, 128),)),
    }


EPSILON = 1e-06
NEGATIVE = -1e+30

def norm_scale(values, gain):
    return values * lax.rsqrt(lax.optimization_barrier(jnp.mean(values * values, axis=-1, keepdims=True)) + EPSILON) * gain

def layout(lengths, count):
    ends = jnp.cumsum(lengths).astype(jnp.int32)
    starts = (ends - lengths).astype(jnp.int32)
    row_ids = jnp.arange(count, dtype=jnp.int32)
    segment = lax.optimization_barrier(jnp.sum((row_ids[:, None] >= ends[None, :]).astype(jnp.int32), axis=1)).astype(jnp.int32)
    total = ends[-1]
    live = row_ids < total
    member = segment[:, None] == jnp.arange(lengths.shape[0], dtype=jnp.int32)[None, :]
    begin = lax.optimization_barrier(jnp.sum(jnp.where(member, starts[None, :], 0), axis=1)).astype(jnp.int32)
    begin = begin + jnp.where(live, 0, total).astype(jnp.int32)
    return (segment, live, (row_ids - begin).astype(jnp.int32), row_ids)

def rotary_tables(position, width):
    half = width // 2
    freqs = 10000.0 ** (-2.0 * jnp.arange(half, dtype=jnp.float32) / width)
    angle = position.astype(jnp.float32)[:, None] * freqs[None, :]
    return (jnp.cos(angle), jnp.sin(angle))

def head_prep(values, gain, cosine, sine):
    normed = norm_scale(values, gain)
    half = values.shape[-1] // 2
    first = normed[..., :half]
    second = normed[..., half:]
    cos_b = cosine[:, None, :]
    sin_b = sine[:, None, :]
    return jnp.concatenate([first * cos_b - second * sin_b, second * cos_b + first * sin_b], axis=-1)

def geglu(gate, up):
    return jax.nn.gelu(gate, approximate=True) * up

def layer_block(block_in, block_len, block_cot, weights, gains):
    q_weight, k_weight, v_weight, o_weight, gate_weight, up_weight, down_weight = weights
    gain_attn, gain_post, gain_mid, gain_last, gain_query, gain_key = gains
    count = block_in.shape[0]
    segment, live, position, row_ids = layout(block_len, count)
    live_col = live.astype(jnp.float32)[:, None]
    cosine, sine = rotary_tables(position, HD)
    same = (segment[:, None] == segment[None, :]) & (row_ids[None, :] <= row_ids[:, None])
    scale = HD ** (-0.5)
    residual = block_in.astype(jnp.float32)
    normed_one = norm_scale(residual, gain_attn).astype(jnp.bfloat16)
    query_acc = jnp.dot(normed_one, q_weight, preferred_element_type=jnp.float32)
    key_acc = jnp.dot(normed_one, k_weight, preferred_element_type=jnp.float32)
    value_b = jnp.dot(normed_one, v_weight, preferred_element_type=jnp.float32).astype(jnp.bfloat16)
    query_heads = query_acc.reshape(count, HEADS, HD)
    key_heads = key_acc.reshape(count, 1, HD)
    query_rot = head_prep(query_heads, gain_query, cosine, sine).astype(jnp.bfloat16)
    key_rot = head_prep(key_heads, gain_key, cosine, sine)[:, 0].astype(jnp.bfloat16)
    scores = jnp.einsum('qhd,kd->hqk', query_rot.astype(jnp.float32), key_rot.astype(jnp.float32)) * scale
    scores = jnp.where(same[None], scores, NEGATIVE)
    peak = lax.optimization_barrier(jnp.max(scores, axis=-1, keepdims=True))
    log_total = peak + jnp.log(lax.optimization_barrier(jnp.sum(jnp.exp(scores - peak), axis=-1, keepdims=True)))
    probs = jnp.exp(scores - log_total)
    probs_b = probs.astype(jnp.bfloat16)
    mixed = jnp.einsum('hqk,kd->qhd', probs_b.astype(jnp.float32), value_b.astype(jnp.float32))
    mixed = mixed.reshape(count, HEADS * HD).astype(jnp.bfloat16)
    attention = jnp.dot(mixed, o_weight.T, preferred_element_type=jnp.float32)
    middle = residual + norm_scale(attention, gain_post)
    normed_two = norm_scale(middle, gain_mid).astype(jnp.bfloat16)
    gate_acc = jnp.dot(normed_two, gate_weight, preferred_element_type=jnp.float32)
    up_acc = jnp.dot(normed_two, up_weight, preferred_element_type=jnp.float32)
    hidden_b = geglu(gate_acc, up_acc).astype(jnp.bfloat16)
    feed = jnp.dot(hidden_b, down_weight.T, preferred_element_type=jnp.float32)
    outputs = ((middle + norm_scale(feed, gain_last)) * live_col).astype(jnp.bfloat16)
    grad_out = block_cot.astype(jnp.float32) * live_col
    unused, pull_last = jax.vjp(norm_scale, feed, gain_last)
    grad_feed, grad_last = pull_last(grad_out)
    feed_b = grad_feed.astype(jnp.bfloat16)
    grad_down = jnp.dot(feed_b.T, hidden_b, preferred_element_type=jnp.float32)
    grad_hidden = jnp.dot(feed_b, down_weight, preferred_element_type=jnp.float32)
    unused, pull_glu = jax.vjp(geglu, gate_acc, up_acc)
    grad_gate, grad_up = pull_glu(grad_hidden)
    gate_b = grad_gate.astype(jnp.bfloat16)
    up_b = grad_up.astype(jnp.bfloat16)
    grad_gate_w = jnp.dot(normed_two.T, gate_b, preferred_element_type=jnp.float32)
    grad_up_w = jnp.dot(normed_two.T, up_b, preferred_element_type=jnp.float32)
    grad_normed = jnp.dot(gate_b, gate_weight.T, preferred_element_type=jnp.float32)
    grad_normed = grad_normed + jnp.dot(up_b, up_weight.T, preferred_element_type=jnp.float32)
    unused, pull_mid = jax.vjp(norm_scale, middle, gain_mid)
    back_mid, grad_mid = pull_mid(grad_normed)
    grad_middle = grad_out + back_mid
    unused, pull_post = jax.vjp(norm_scale, attention, gain_post)
    grad_attention, grad_post = pull_post(grad_middle)
    attention_b = grad_attention.astype(jnp.bfloat16)
    grad_o = jnp.dot(attention_b.T, mixed, preferred_element_type=jnp.float32)
    grad_mixed = jnp.dot(attention_b, o_weight, preferred_element_type=jnp.float32).astype(jnp.bfloat16)
    grad_mixed = grad_mixed.reshape(count, HEADS, HD).astype(jnp.float32)
    grad_probs = jnp.einsum('qhd,kd->hqk', grad_mixed, value_b.astype(jnp.float32))
    inner = lax.optimization_barrier(jnp.sum(probs * grad_probs, axis=-1, keepdims=True))
    grad_scores = (probs * (grad_probs - inner) * scale).astype(jnp.bfloat16).astype(jnp.float32)
    grad_qrot = jnp.einsum('hqk,kd->qhd', grad_scores, key_rot.astype(jnp.float32))
    grad_krot = jnp.einsum('hqk,qhd->kd', grad_scores, query_rot.astype(jnp.float32))
    grad_value = jnp.einsum('hqk,qhd->kd', probs_b.astype(jnp.float32), grad_mixed)
    unused, pull_query = jax.vjp(lambda values, gain: head_prep(values, gain, cosine, sine), query_heads, gain_query)
    grad_query, grad_qgain = pull_query(grad_qrot)
    unused, pull_key = jax.vjp(lambda values, gain: head_prep(values, gain, cosine, sine), key_heads, gain_key)
    grad_key, grad_kgain = pull_key(grad_krot[:, None, :])
    query_b = grad_query.reshape(count, HEADS * HD).astype(jnp.bfloat16)
    key_b = grad_key.reshape(count, HD).astype(jnp.bfloat16)
    value_grad_b = grad_value.astype(jnp.bfloat16)
    grad_q = jnp.dot(normed_one.T, query_b, preferred_element_type=jnp.float32)
    grad_k = jnp.dot(normed_one.T, key_b, preferred_element_type=jnp.float32)
    grad_v = jnp.dot(normed_one.T, value_grad_b, preferred_element_type=jnp.float32)
    grad_first_in = jnp.dot(query_b, q_weight.T, preferred_element_type=jnp.float32)
    grad_first_in = grad_first_in + jnp.dot(key_b, k_weight.T, preferred_element_type=jnp.float32)
    grad_first_in = grad_first_in + jnp.dot(value_grad_b, v_weight.T, preferred_element_type=jnp.float32)
    unused, pull_first = jax.vjp(norm_scale, residual, gain_attn)
    back_first, grad_first = pull_first(grad_first_in)
    input_grad = (grad_middle + back_first).astype(jnp.bfloat16)
    grads = (grad_q, grad_k, grad_v, grad_o, grad_gate_w, grad_up_w, grad_down, grad_first, grad_post, grad_mid, grad_last, grad_qgain, grad_kgain)
    return (outputs, input_grad, grads)

def reference(inputs, lengths, q_weight, k_weight, v_weight, o_weight, gate_weight, up_weight, down_weight, attn_norm, attn_post_norm, mlp_norm, mlp_post_norm, query_norm, key_norm, cotangent):
    weights = (q_weight, k_weight, v_weight, o_weight, gate_weight, up_weight, down_weight)
    gains = (attn_norm.astype(jnp.float32), attn_post_norm.astype(jnp.float32), mlp_norm.astype(jnp.float32), mlp_post_norm.astype(jnp.float32), query_norm.astype(jnp.float32), key_norm.astype(jnp.float32))
    shapes = [(D, HEADS * HD), (D, HD), (D, HD), (D, HEADS * HD), (D, FF), (D, FF), (D, FF), (D,), (D,), (D,), (D,), (HD,), (HD,)]
    start_grads = tuple((jnp.zeros(shape, jnp.float32) for shape in shapes))
    blocks = (inputs.reshape(DEVICES, TOK_DEV, D), lengths, cotangent.reshape(DEVICES, TOK_DEV, D))

    def step(carry, block):
        outputs, input_grad, grads = layer_block(block[0], block[1], block[2], weights, gains)
        return (tuple((old + new for old, new in zip(carry, grads))), (outputs, input_grad))
    totals, produced = lax.scan(step, start_grads, blocks)
    return (produced[0].reshape(ROWS, D), produced[1].reshape(ROWS, D), totals[0], totals[1], totals[2], totals[3], totals[4], totals[5], totals[6], totals[7], totals[8], totals[9], totals[10], totals[11], totals[12])
```

```python
import jax
import jax.numpy as jnp
from jax import lax
from jax.sharding import PartitionSpec as P


EPSILON = 1e-06
NEGATIVE = -1e30


def norm_scale(values, gain):
    return values * lax.rsqrt(jnp.mean(values * values, axis=-1, keepdims=True) + EPSILON) * gain


def unit_rows(values):
    return values * lax.rsqrt(jnp.mean(values * values, axis=-1, keepdims=True) + EPSILON)


def layout(lengths, count):
    ends = jnp.cumsum(lengths)
    starts = ends - lengths
    row_ids = jnp.arange(count, dtype=jnp.int32)
    segment = jnp.sum((row_ids[:, None] >= ends[None, :]).astype(jnp.int32), axis=1)
    total = ends[-1]
    live = row_ids < total
    member = segment[:, None] == jnp.arange(lengths.shape[0], dtype=jnp.int32)[None, :]
    begin = jnp.sum(jnp.where(member, starts[None, :], 0), axis=1)
    begin = begin + jnp.where(live, 0, total)
    return (segment, live, row_ids - begin, row_ids)


def rotary_tables(position, width):
    half = width // 2
    freqs = 10000.0 ** (-2.0 * jnp.arange(half, dtype=jnp.float32) / width)
    angle = position.astype(jnp.float32)[:, None] * freqs[None, :]
    return (jnp.cos(angle), jnp.sin(angle))


def head_prep(values, gain, cosine, sine):
    normed = norm_scale(values, gain)
    half = values.shape[-1] // 2
    first = normed[..., :half]
    second = normed[..., half:]
    cos_b = cosine[:, None, :]
    sin_b = sine[:, None, :]
    return jnp.concatenate(
        [first * cos_b - second * sin_b, second * cos_b + first * sin_b], axis=-1
    )


def geglu(gate, up):
    return jax.nn.gelu(gate, approximate=True) * up


def dot_rows(left, right):
    return lax.dot_general(
        left, right, (((1,), (1,)), ((), ())), preferred_element_type=jnp.float32
    )


def dot_cols(left, right):
    return lax.dot_general(
        left, right, (((0,), (0,)), ((), ())), preferred_element_type=jnp.float32
    )


def gather_rep(block):
    size = lax.axis_size("rep")
    same = [block]
    for step in range(2, size, 2):
        same.append(lax.ppermute(block, "rep", [(i, (i + step) % size) for i in range(size)]))
    mine = jnp.concatenate(same, axis=0)
    other = lax.ppermute(mine, "rep", [(i, i ^ 1) for i in range(size)])
    return jnp.concatenate([mine, other], axis=0)


def scatter_rep(partial):
    size = lax.axis_size("rep")
    half = partial.shape[0] // 2
    count = half // (size // 2)
    swapped = lax.ppermute(
        partial[half:].astype(jnp.bfloat16), "rep", [(i, i ^ 1) for i in range(size)]
    )
    both = partial[:half].astype(jnp.float32) + swapped.astype(jnp.float32)
    total = both[:count]
    for index in range(1, size // 2):
        piece = both[index * count : (index + 1) * count].astype(jnp.bfloat16)
        moved = lax.ppermute(
            piece, "rep", [(i, (i - 2 * index) % size) for i in range(size)]
        )
        total = total + moved.astype(jnp.float32)
    return total


def sum_rep(values):
    size = lax.axis_size("rep")
    bit = 1
    total = values
    while bit < size:
        moved = lax.ppermute(total, "rep", [(i, i ^ bit) for i in range(size)])
        wide = total.astype(jnp.float32) + moved.astype(jnp.float32)
        bit *= 2
        total = wide.astype(jnp.bfloat16)
    return total.astype(jnp.float32)


def per_device(
    inputs,
    lengths,
    q_weight,
    k_weight,
    v_weight,
    o_weight,
    gate_weight,
    up_weight,
    down_weight,
    attn_norm,
    attn_post_norm,
    mlp_norm,
    mlp_post_norm,
    query_norm,
    key_norm,
    cotangent,
):
    bf16 = jnp.bfloat16
    f32 = jnp.float32
    count, width = inputs.shape
    groups = lax.axis_size("shard")
    replicas = lax.axis_size("rep")
    rep = lax.axis_index("rep")
    rows = q_weight.shape[0]
    head_local = query_norm.shape[0]
    head_width = head_local * groups
    q_width = q_weight.shape[1]
    ff_width = gate_weight.shape[1]
    heads = q_width // head_width
    scale = head_width ** (-0.5)
    key_end = q_width + head_width
    value_end = q_width + 2 * head_width
    part = ff_width // replicas
    padded = -(-part // 128) * 128

    def column(vector):
        return jnp.pad(vector, (0, rows - vector.shape[0]))[:, None]

    small = jnp.concatenate(
        [column(v) for v in (attn_norm, attn_post_norm, mlp_norm, mlp_post_norm, query_norm, key_norm)],
        axis=1,
    )
    small = jnp.pad(small, ((0, 0), (0, 122)))
    first_pack = jnp.concatenate([q_weight, k_weight, v_weight, small], axis=1)

    def own(weight):
        piece = lax.dynamic_slice_in_dim(weight, rep * part, part, axis=1)
        return jnp.pad(piece, ((0, 0), (0, padded - part)))

    full_first = lax.all_gather(first_pack, "shard", axis=0, tiled=True)
    full_o = lax.all_gather(o_weight, "shard", axis=0, tiled=True)
    full_branch = lax.all_gather(
        jnp.concatenate([own(gate_weight), own(up_weight)], axis=1), "shard", axis=0, tiled=True
    )
    full_down = lax.all_gather(own(down_weight), "shard", axis=0, tiled=True)

    segment, live, position, row_ids = layout(lengths[0], count)
    live_col = live.astype(f32)[:, None]
    cosine, sine = rotary_tables(position, head_width)
    same = (segment[:, None] == segment[None, :]) & (row_ids[None, :] <= row_ids[:, None])
    residual = inputs.astype(f32)
    unit_one = unit_rows(residual)
    gains = full_first[:, value_end : value_end + 8].astype(f32).T
    gain_attn, gain_post, gain_mid, gain_last = gains[0], gains[1], gains[2], gains[3]
    gain_query = gains[4].reshape(groups, rows)[:, :head_local].reshape(head_width)
    gain_key = gains[5].reshape(groups, rows)[:, :head_local].reshape(head_width)

    normed_one = (unit_one * gain_attn).astype(bf16)
    first = jnp.dot(normed_one, full_first, preferred_element_type=f32)
    query_heads = first[:, :q_width].reshape(count, heads, head_width)
    key_heads = first[:, q_width:key_end].reshape(count, 1, head_width)
    value_b = first[:, key_end:value_end].astype(bf16)
    query_rot = head_prep(query_heads, gain_query, cosine, sine).astype(bf16)
    key_rot = head_prep(key_heads, gain_key, cosine, sine)[:, 0].astype(bf16)
    raw = jnp.einsum("qhd,kd->hqk", query_rot, key_rot, preferred_element_type=f32) * scale
    scores = jnp.where(same[None], raw, NEGATIVE)
    peak = jnp.max(scores, axis=-1, keepdims=True)
    log_total = peak + jnp.log(jnp.sum(jnp.exp(scores - peak), axis=-1, keepdims=True))
    probs = jnp.exp(scores - log_total)
    probs_b = probs.astype(bf16)
    mixed = jnp.einsum("hqk,kd->qhd", probs_b, value_b, preferred_element_type=f32)
    mixed = mixed.reshape(count, q_width).astype(bf16)
    attention = dot_rows(mixed, full_o)
    middle = residual + norm_scale(attention, gain_post)
    normed_two = (unit_rows(middle) * gain_mid).astype(bf16)

    all_two = gather_rep(normed_two)
    branch = jnp.dot(all_two, full_branch, preferred_element_type=f32)
    gate_acc, up_acc = branch[:, :padded], branch[:, padded:]
    hidden_b = geglu(gate_acc, up_acc).astype(bf16)
    feed = scatter_rep(dot_rows(hidden_b, full_down).astype(bf16))
    outputs = ((middle + norm_scale(feed, gain_last)) * live_col).astype(bf16)

    grad_out = cotangent.astype(f32) * live_col
    unused, pull_last = jax.vjp(norm_scale, feed, gain_last)
    grad_feed, grad_last = pull_last(grad_out)
    all_feed = gather_rep(grad_feed.astype(bf16))
    grad_hidden = jnp.dot(all_feed, full_down, preferred_element_type=f32)
    unused, pull_glu = jax.vjp(geglu, gate_acc, up_acc)
    grad_gate, grad_up = pull_glu(grad_hidden)
    branch_grads = jnp.concatenate([grad_gate.astype(bf16), grad_up.astype(bf16)], axis=1)
    grad_normed = scatter_rep(dot_rows(branch_grads, full_branch).astype(bf16))
    down_sum = lax.psum_scatter(
        dot_cols(all_feed, hidden_b).astype(bf16), "shard", scatter_dimension=0, tiled=True
    )
    branch_sum = lax.psum_scatter(
        dot_cols(all_two, branch_grads).astype(bf16), "shard", scatter_dimension=0, tiled=True
    )
    mlp_all = lax.all_gather(jnp.concatenate([branch_sum, down_sum], axis=1), "rep", axis=0)

    def whole(start):
        piece = mlp_all[:, :, start : start + part].astype(f32)
        return jnp.concatenate([piece[i] for i in range(replicas)], axis=1)

    unused, pull_mid = jax.vjp(norm_scale, middle, gain_mid)
    back_mid, grad_mid = pull_mid(grad_normed)
    grad_middle = grad_out + back_mid
    unused, pull_post = jax.vjp(norm_scale, attention, gain_post)
    grad_attention, grad_post = pull_post(grad_middle)
    attention_b = grad_attention.astype(bf16)
    grad_mixed = jnp.dot(attention_b, full_o, preferred_element_type=f32).astype(bf16)
    grad_mixed = grad_mixed.reshape(count, heads, head_width)
    grad_probs = jnp.einsum("qhd,kd->hqk", grad_mixed, value_b, preferred_element_type=f32)
    inner = jnp.sum(probs * grad_probs, axis=-1, keepdims=True)
    grad_scores = (probs * (grad_probs - inner) * scale).astype(bf16)
    grad_qrot = jnp.einsum("hqk,kd->qhd", grad_scores, key_rot, preferred_element_type=f32)
    grad_krot = jnp.einsum("hqk,qhd->kd", grad_scores, query_rot, preferred_element_type=f32)
    grad_value = jnp.einsum("hqk,qhd->kd", probs_b, grad_mixed, preferred_element_type=f32)
    unused, pull_query = jax.vjp(
        lambda values, gain: head_prep(values, gain, cosine, sine), query_heads, gain_query
    )
    grad_query, grad_qgain = pull_query(grad_qrot)
    unused, pull_key = jax.vjp(
        lambda values, gain: head_prep(values, gain, cosine, sine), key_heads, gain_key
    )
    grad_key, grad_kgain = pull_key(grad_krot[:, None, :])
    projected = jnp.concatenate(
        [
            grad_query.reshape(count, q_width).astype(bf16),
            grad_key.reshape(count, head_width).astype(bf16),
            grad_value.astype(bf16),
            jnp.zeros((count, 128), bf16),
        ],
        axis=1,
    )
    grad_first_in = dot_rows(projected, full_first)
    unused, pull_first = jax.vjp(norm_scale, residual, gain_attn)
    back_first, grad_first = pull_first(grad_first_in)
    input_grad = (grad_middle + back_first).astype(bf16)

    def spread(vector):
        return jnp.pad(vector.reshape(groups, head_local), ((0, 0), (0, rows - head_local))).reshape(width)

    gain_grads = jnp.stack(
        [grad_first, grad_post, grad_mid, grad_last, spread(grad_qgain), spread(grad_kgain)]
        + [jnp.zeros_like(grad_first)] * 2
    ).astype(bf16)
    gain_cols = jnp.pad(gain_grads.T, ((0, 0), (0, 120)))
    left = dot_cols(normed_one, projected[:, :value_end]).astype(bf16)
    right = dot_cols(attention_b, mixed).astype(bf16)
    attn_sum = lax.psum_scatter(
        jnp.concatenate([left, right, gain_cols], axis=1), "shard", scatter_dimension=0, tiled=True
    )
    total = sum_rep(attn_sum)
    o_end = value_end + q_width
    small_total = total[:, o_end : o_end + 8].T
    return (
        outputs,
        input_grad,
        total[:, :q_width],
        total[:, q_width:key_end],
        total[:, key_end:value_end],
        total[:, value_end:o_end],
        whole(0),
        whole(padded),
        whole(2 * padded),
        small_total[0],
        small_total[1],
        small_total[2],
        small_total[3],
        small_total[4, :head_local],
        small_total[5, :head_local],
    )


def solution(mesh):
    in_specs = (
        P(("rep", "shard"), None),
        P(("rep", "shard"), None),
        P("shard", None),
        P("shard", None),
        P("shard", None),
        P("shard", None),
        P("shard", None),
        P("shard", None),
        P("shard", None),
        P("shard"),
        P("shard"),
        P("shard"),
        P("shard"),
        P("shard"),
        P("shard"),
        P(("rep", "shard"), None),
    )
    out_specs = (
        P(("rep", "shard"), None),
        P(("rep", "shard"), None),
        P("shard", None),
        P("shard", None),
        P("shard", None),
        P("shard", None),
        P("shard", None),
        P("shard", None),
        P("shard", None),
        P("shard"),
        P("shard"),
        P("shard"),
        P("shard"),
        P("shard"),
        P("shard"),
    )
    return jax.shard_map(
        per_device, mesh=mesh, in_specs=in_specs, out_specs=out_specs, check_vma=False
    )
```
